32 devices in a mesh: wide: 8 (over z, y), narrow: 4 (over x, core).
Axes of the slice: x: 2, y: 2, z: 4, core: 2. Of those that a mesh axis runs over, the one named last changes fastest.
Arguments:
- frames: bfloat16 [256, 2, 256, 256], P(('wide', 'narrow')), may hold values from -120 to 120
- sketch: bfloat16 [256, 128], replicated, may hold values from -0.3 to 2.3
- kernel_taps: bfloat16 [64], replicated, may hold values from -0.3 to 1.1
Outputs:
- basis: float32 [128, 32768], P(None, ('wide', 'narrow'))
- factor: float32 [128, 128], replicated
The draws below stay inside these ranges and needn't reach their ends.
All inputs are finite; a program needn't handle non-finite values.
Results may differ from the reference program's by a relative error of at most 0.0043.
Values may be sent and summed in bfloat16 or wider, within the bound.
No kernel may reach another device: no remote copies, remote signals or barrier semaphores. Data moves between devices by JAX's collectives and lax.ppermute only.
A program may use at most 64 MiB of HBM per device.

```python
import math
import jax
import jax.numpy as jnp
from jax import lax

PLANES = 2
ROWS = 256
COLS = 256
TIME = 256
RANK = 128
NTAP = 64
VOXELS = 32768


def draw_frames(key, part):
    key_noise, key_rows, key_times = jax.random.split(key, 3)
    layout = (TIME, PLANES, ROWS, COLS)
    noise = jax.random.truncated_normal(key_noise, -4.0, 4.0, layout, jnp.float32)
    row_scale = jnp.exp(jax.random.uniform(key_rows, (1, PLANES, ROWS, 1), jnp.float32, 0.0, math.log(10.0)))
    time_scale = jnp.exp(jax.random.uniform(key_times, (TIME, 1, 1, 1), jnp.float32, 0.0, math.log(2.0)))
    values = noise * row_scale * time_scale
    return values.astype(jnp.bfloat16)


def draw_sketch(key, part):
    spread = 1.0 / (math.sqrt(TIME) + math.sqrt(RANK))
    random_part = jax.random.truncated_normal(key, -4.0, 4.0, (TIME, RANK), jnp.float32) * spread
    diagonal = jnp.arange(TIME, dtype=jnp.int32)[:, None] == jnp.arange(RANK, dtype=jnp.int32)[None, :]
    return (random_part + jnp.where(diagonal, jnp.float32(2.0), jnp.float32(0.0))).astype(jnp.bfloat16)


def draw_kernel_taps(key, part):
    key_lead, key_rest = jax.random.split(key, 2)
    position = jnp.arange(NTAP, dtype=jnp.float32)
    weights = jnp.exp(-(position - 1.0) / 16.0) / 16.5
    rest = jax.random.uniform(key_rest, (NTAP,), jnp.float32, -1.0, 1.0) * 0.3 * weights
    lead = jax.random.uniform(key_lead, (NTAP,), jnp.float32, 0.9, 1.1)
    return jnp.where(position < 0.5, lead, rest).astype(jnp.bfloat16)


def setup_inputs(seed: int = 0) -> dict:
    streams_of = jax.random.split(jax.random.key(seed), 4)
    return {
        "frames": draw_frames(jax.random.fold_in(streams_of[3], 71), 0),
        "sketch": draw_sketch(jax.random.fold_in(streams_of[3], 71), 0),
        "kernel_taps": draw_kernel_taps(jax.random.fold_in(streams_of[3], 71), 0),
    }


def gauss_taps(spread):
    position = jnp.arange(15, dtype=jnp.float32) - 7.0
    weights = jnp.exp(-position * position / (2.0 * spread * spread))
    return weights / jnp.sum(weights)

def band_matrix(spread, length):
    outputs = length // 2
    offset_index = jnp.arange(length, dtype=jnp.int32)[None, :] - 2 * jnp.arange(outputs, dtype=jnp.int32)[:, None] + 7
    weights = gauss_taps(spread)
    matrix = jnp.zeros((outputs, length), jnp.float32)
    for offset in range(15):
        matrix = matrix + jnp.where(offset_index == offset, weights[offset], jnp.float32(0.0))
    return matrix

def filter_volumes(frames_block):
    volume = frames_block.astype(jnp.float32)
    row_count = volume.shape[-2]
    col_count = volume.shape[-1]
    half = col_count // 2
    column_bands = jnp.concatenate([band_matrix(1.5, col_count), band_matrix(3.0, col_count)], axis=0)
    column_pass = jnp.einsum('...rc,oc->...ro', volume, column_bands, precision=lax.Precision.HIGHEST)
    narrow_pass = jnp.einsum('or,...rc->...oc', band_matrix(1.5, row_count), column_pass[..., :half], precision=lax.Precision.HIGHEST)
    broad_pass = jnp.einsum('or,...rc->...oc', band_matrix(3.0, row_count), column_pass[..., half:], precision=lax.Precision.HIGHEST)
    return (narrow_pass - broad_pass).astype(jnp.bfloat16)

def build_toeplitz(kernel_taps, length):
    lag_index = jnp.arange(length, dtype=jnp.int32)[:, None] - jnp.arange(length, dtype=jnp.int32)[None, :]
    toeplitz = jnp.zeros((length, length), jnp.float32)
    for offset in range(kernel_taps.shape[0]):
        toeplitz = toeplitz + jnp.where(lag_index == offset, kernel_taps[offset].astype(jnp.float32), jnp.float32(0.0))
    return toeplitz.astype(jnp.bfloat16)

def orthonormalize(sketched, voxel_count):
    gram_part = lax.dot_general(sketched.astype(jnp.float32), sketched.astype(jnp.float32), (((1,), (1,)), ((), ())), precision=lax.Precision.HIGHEST, preferred_element_type=jnp.float32) / voxel_count
    lower_factor = jnp.linalg.cholesky(gram_part)
    basis_rows = jax.scipy.linalg.solve_triangular(lower_factor, sketched, lower=True)
    return (basis_rows, lower_factor.T)

def reference(frames, sketch, kernel_taps):
    filtered = lax.map(filter_volumes, frames).reshape(TIME, VOXELS)
    toeplitz = build_toeplitz(kernel_taps, TIME)
    deconvolved = jnp.dot(toeplitz.astype(jnp.float32), filtered.astype(jnp.float32), preferred_element_type=jnp.float32).astype(jnp.bfloat16)
    sketched = lax.dot_general(sketch.astype(jnp.float32), deconvolved.astype(jnp.float32), (((0,), (0,)), ((), ())), preferred_element_type=jnp.float32)
    first_basis, unused = orthonormalize(sketched, VOXELS)
    series = deconvolved.astype(jnp.float32)
    projected = lax.dot_general(series.astype(jnp.float32), first_basis.astype(jnp.float32), (((1,), (1,)), ((), ())), precision=lax.Precision.HIGHEST, preferred_element_type=jnp.float32) / VOXELS
    refined = lax.dot_general(projected.astype(jnp.float32), series.astype(jnp.float32), (((0,), (0,)), ((), ())), precision=lax.Precision.HIGHEST, preferred_element_type=jnp.float32)
    basis, factor = orthonormalize(refined, VOXELS)
    return (basis, factor)
```

```python
import functools

import jax
import jax.numpy as jnp
import numpy as np
from jax import lax
from jax.experimental import pallas as pl
from jax.experimental.pallas import tpu as pltpu
from jax.sharding import PartitionSpec as P

AXES = ("wide", "narrow")
SUB = 8
LANES = 128


def gauss_taps(spread):
    position = np.arange(15, dtype=np.float32) - np.float32(7.0)
    weights = np.exp(-position * position / np.float32(2.0 * spread * spread))
    return (weights / np.sum(weights, dtype=np.float32)).astype(np.float32)


def band_matrix(spread, length):
    outputs = length // 2
    offset = np.arange(length)[None, :] - 2 * np.arange(outputs)[:, None] + 7
    weights = gauss_taps(spread)
    inside = (offset >= 0) & (offset < 15)
    return np.where(inside, weights[np.clip(offset, 0, 14)], np.float32(0.0))


def split_constant(matrix):
    high = matrix.astype(jnp.bfloat16)
    low = (matrix - high.astype(np.float32)).astype(jnp.bfloat16)
    return high, low


def dot(left, right, contract=((1,), (0,))):
    return lax.dot_general(left, right, (contract, ((), ())), preferred_element_type=jnp.float32)


def exact_dot(left, right, contract=((1,), (0,))):
    return lax.dot_general(
        left,
        right,
        (contract, ((), ())),
        precision=lax.Precision.HIGHEST,
        preferred_element_type=jnp.float32,
    )


def split(value, parts):
    pieces = []
    for _ in range(parts):
        piece = value.astype(jnp.bfloat16)
        pieces.append(piece)
        value = value - piece.astype(jnp.float32)
    return pieces


def filter_kernel(frames, row_bands, col_bands, out, held, planes, sems):
    count, plane_count = frames.shape[0], frames.shape[1]
    half_rows, half_cols = row_bands.shape[0] // 4, col_bands.shape[1] // 2
    copies = []
    for t in range(count):
        copy = pltpu.make_async_copy(frames.at[t], held.at[t], sems.at[t])
        copy.start()
        copies.append(copy)
    for t in range(count):
        copies[t].wait()
        narrow, broad = [], []
        for p in range(plane_count):
            passed = dot(row_bands[...], held[t, p])
            both = passed[: 2 * half_rows] + passed[2 * half_rows :]
            narrow.append(both[:half_rows])
            broad.append(both[half_rows:])
        narrow = jnp.concatenate(narrow, axis=0)
        broad = jnp.concatenate(broad, axis=0)
        length = narrow.shape[1]
        parts = zip(split(narrow, 2), split(broad, 2))
        (narrow_high, broad_high), (narrow_low, broad_low) = parts
        wide_sum = dot(narrow_high, col_bands[:length]) + dot(broad_high, col_bands[length:])
        low_sum = dot(narrow_low, col_bands[:length, :half_cols]) + dot(
            broad_low, col_bands[length:, :half_cols]
        )
        planes[:, t, :] = wide_sum[:, :half_cols] + (wide_sum[:, half_cols:] + low_sum)
    out[...] = planes[...].astype(jnp.bfloat16).reshape(out.shape)


def filter_call(frames, groups):
    count, plane_count, rows, cols = frames.shape
    narrow_high, narrow_low = split_constant(band_matrix(1.5, rows))
    broad_high, broad_low = split_constant(band_matrix(3.0, rows))
    row_bands = np.concatenate([narrow_high, broad_high, narrow_low, broad_low], axis=0)
    narrow_high, narrow_low = split_constant(band_matrix(1.5, cols).T)
    broad_high, broad_low = split_constant(-band_matrix(3.0, cols).T)
    col_bands = np.concatenate(
        [
            np.concatenate([narrow_high, narrow_low], axis=1),
            np.concatenate([broad_high, broad_low], axis=1),
        ],
        axis=0,
    )
    lines = plane_count * (rows // 2)
    shape = (groups, lines // groups, count, cols // 2)
    vmem = pl.BlockSpec(memory_space=pltpu.VMEM)
    return pl.pallas_call(
        filter_kernel,
        out_shape=jax.ShapeDtypeStruct(shape, jnp.bfloat16),
        in_specs=[pl.BlockSpec(memory_space=pl.ANY), vmem, vmem],
        out_specs=vmem,
        scratch_shapes=[
            pltpu.VMEM(frames.shape, jnp.bfloat16),
            pltpu.VMEM((lines, count, cols // 2), jnp.float32),
            pltpu.SemaphoreType.DMA((count,)),
        ],
        name="filter_volumes",
    )(frames, jnp.asarray(row_bands), jnp.asarray(col_bands))


def deconvolve_kernel(voxel_count, taps, received, deconvolved, gram):
    length = deconvolved.shape[0]
    taps_row = jnp.concatenate(
        [taps[...].astype(jnp.float32), jnp.zeros((1, length - taps.shape[1]), jnp.float32)], axis=1
    )
    lags = pltpu.roll(
        jnp.broadcast_to(taps_row, (length, length)), 0, 1, stride=1, stride_axis=0
    )
    source = lax.broadcasted_iota(jnp.int32, (length, length), 0)
    target = lax.broadcasted_iota(jnp.int32, (length, length), 1)
    toeplitz = jnp.where(target >= source, lags, 0.0).T.astype(jnp.bfloat16)
    if len(received.shape) == 4:
        lines = [
            received[:, r].astype(jnp.float32).reshape(length, received.shape[3]).astype(jnp.bfloat16)
            for r in range(received.shape[1])
        ]
    else:
        lines = [received[r] for r in range(received.shape[0])]
    series = dot(toeplitz, jnp.concatenate(lines, axis=1)).astype(jnp.bfloat16)
    deconvolved[...] = series
    full = dot(series, series, ((1,), (1,))) * (1.0 / voxel_count)
    half = length // 2
    gram[:half] = full[:half, :half]
    gram[half:length] = full[half:, :half]
    gram[length:] = full[half:, half:]


def deconvolve_call(kernel_taps, received, voxel_count):
    groups, lines, count, width = received.shape
    length = groups * count
    if count % SUB:
        received = jnp.swapaxes(received, 0, 1).reshape(lines, length, width)
    vmem = pl.BlockSpec(memory_space=pltpu.VMEM)
    return pl.pallas_call(
        functools.partial(deconvolve_kernel, voxel_count),
        out_shape=(
            jax.ShapeDtypeStruct((length, lines * width), jnp.bfloat16),
            jax.ShapeDtypeStruct((length + length // 2, length // 2), jnp.float32),
        ),
        in_specs=[vmem, vmem],
        out_specs=(vmem, vmem),
        name="deconvolve_gram",
    )(kernel_taps.reshape(1, -1), received)


def exchange(value, mask, size):
    return lax.ppermute(value, AXES, [(i, i ^ mask) for i in range(size)])


def sum_over_devices(packed, size):
    bits = size.bit_length() - 1
    rows = packed.shape[0] // 2
    start = (lax.axis_index(AXES) % 2) * rows
    other = exchange(packed, 1, size)
    half = lax.dynamic_slice_in_dim(packed, start, rows) + lax.dynamic_slice_in_dim(
        other, start, rows
    )
    first = [exchange(half, mask, size) for mask in (2, 4, 6)]
    half = (half + first[0]) + (first[1] + first[2])
    bit = 3
    while bit < bits:
        half = half + exchange(half, 1 << bit, size)
        if bit + 1 < bits:
            half = half + exchange(half, 3 << bit, size)
        bit += 2
    return half, exchange(half, 1, size)


def eliminate(gram):
    size = gram.shape[0]
    blocks = size // SUB
    identity = (
        lax.broadcasted_iota(jnp.int32, (size, size), 0)
        == lax.broadcasted_iota(jnp.int32, (size, size), 1)
    ).astype(jnp.float32)
    left = [gram[SUB * i : SUB * (i + 1)] for i in range(blocks)]
    right = [identity[SUB * i : SUB * (i + 1)] for i in range(blocks)]
    row = lax.broadcasted_iota(jnp.int32, (SUB, size), 0)
    lane = lax.broadcasted_iota(jnp.int32, (SUB, size), 1)

    def columns(block, k):
        return [
            jnp.broadcast_to(block[:, SUB * k + j : SUB * k + j + 1], (SUB, size))
            for j in range(SUB)
        ]

    upper, inverse = [], []
    for k in range(blocks):
        cols = columns(left[k], k)
        steps = []
        pivots = jnp.ones((SUB, size), jnp.float32)
        for j in range(SUB):
            pivot = jnp.broadcast_to(cols[j][j : j + 1], (SUB, size))
            reciprocal = 1.0 / pivot
            pivots = jnp.where(row == j, pivot, pivots)
            tops = [
                jnp.broadcast_to(cols[jj][j : j + 1], (SUB, size)) for jj in range(j + 1, SUB)
            ]
            left_row = jnp.broadcast_to(left[k][j : j + 1], (SUB, size))
            right_row = jnp.broadcast_to(right[k][j : j + 1], (SUB, size))
            ratio = jnp.where(row > j, cols[j] * reciprocal, 0.0)
            for jj in range(j + 1, SUB):
                cols[jj] = cols[jj] - ratio * tops[jj - j - 1]
            left[k] = left[k] - ratio * left_row
            right[k] = right[k] - ratio * right_row
            steps.append((reciprocal, tops, left_row, right_row))
        scale = lax.rsqrt(pivots)
        upper.append(jnp.where(lane >= row + SUB * k, left[k] * scale, 0.0))
        inverse.append(right[k] * scale)
        for i in range(k + 1, blocks):
            cols = columns(left[i], k)
            for j, (reciprocal, tops, left_row, right_row) in enumerate(steps):
                ratio = cols[j] * reciprocal
                for jj in range(j + 1, SUB):
                    cols[jj] = cols[jj] - ratio * tops[jj - j - 1]
                left[i] = left[i] - ratio * left_row
                right[i] = right[i] - ratio * right_row
    return jnp.concatenate(upper, axis=0), jnp.concatenate(inverse, axis=0)


def basis_kernel(lower_half, upper_half, sketch, deconvolved, basis, factor):
    half = lower_half.shape[1]
    rows = lower_half.shape[0]
    packed = jnp.concatenate([lower_half[...], upper_half[...]], axis=0)
    corner = packed[half : 2 * half]
    data_gram = jnp.concatenate(
        [
            jnp.concatenate([packed[:half], corner.T], axis=1),
            jnp.concatenate([corner, packed[2 * half :]], axis=1),
        ],
        axis=0,
    )
    weights = sketch[...]
    high, middle, low = split(data_gram, 3)
    weighted = dot(high, weights) + (dot(middle, weights) + dot(low, weights))
    high, middle, low = split(weighted, 3)
    rows_first = ((0,), (0,))
    gram = dot(weights, high, rows_first) + (
        dot(weights, middle, rows_first) + dot(weights, low, rows_first)
    )
    _, inverse = eliminate(gram)
    projected = exact_dot(inverse, weighted, ((1,), (1,)))
    gram = exact_dot(exact_dot(projected, data_gram), projected, ((1,), (1,)))
    upper, inverse = eliminate(gram)
    factor[...] = upper
    high, middle, low = split(exact_dot(inverse, projected), 3)
    series = deconvolved[...]
    basis[...] = dot(high, series) + (dot(middle, series) + dot(low, series))


def basis_call(lower_half, upper_half, sketch, deconvolved):
    rank = sketch.shape[1]
    vmem = pl.BlockSpec(memory_space=pltpu.VMEM)
    return pl.pallas_call(
        basis_kernel,
        out_shape=(
            jax.ShapeDtypeStruct((rank, deconvolved.shape[1]), jnp.float32),
            jax.ShapeDtypeStruct((rank, rank), jnp.float32),
        ),
        in_specs=[vmem] * 4,
        out_specs=(vmem, vmem),
        name="orthonormal_basis",
    )(lower_half, upper_half, sketch, deconvolved)


def shards(size, frames, sketch, kernel_taps):
    voxel_count = frames.shape[1] * (frames.shape[2] // 2) * (frames.shape[3] // 2)
    filtered = filter_call(frames, size)
    received = lax.all_to_all(filtered, AXES, split_axis=0, concat_axis=0, tiled=True)
    deconvolved, packed = deconvolve_call(kernel_taps, received, voxel_count)
    mine, pairs = sum_over_devices(packed, size)
    second = lax.axis_index(AXES) % 2 == 1
    lower_half = jnp.where(second, pairs, mine)
    upper_half = jnp.where(second, mine, pairs)
    return basis_call(lower_half, upper_half, sketch, deconvolved)


def solution(mesh):
    size = mesh.shape["wide"] * mesh.shape["narrow"]
    return jax.shard_map(
        functools.partial(shards, size),
        mesh=mesh,
        in_specs=(P(AXES, None, None, None), P(), P()),
        out_specs=(P(None, AXES), P()),
        check_vma=False,
    )
```

```python
import functools

import jax
import jax.numpy as jnp
import numpy as np
from jax import lax
from jax.experimental import pallas as pl
from jax.experimental.pallas import tpu as pltpu
from jax.sharding import PartitionSpec as P

AXES = ("wide", "narrow")
SUB = 8
LANES = 128


def gauss_taps(spread):
    position = np.arange(15, dtype=np.float32) - np.float32(7.0)
    weights = np.exp(-position * position / np.float32(2.0 * spread * spread))
    return (weights / np.sum(weights, dtype=np.float32)).astype(np.float32)


def band_matrix(spread, length):
    outputs = length // 2
    offset = np.arange(length)[None, :] - 2 * np.arange(outputs)[:, None] + 7
    weights = gauss_taps(spread)
    inside = (offset >= 0) & (offset < 15)
    return np.where(inside, weights[np.clip(offset, 0, 14)], np.float32(0.0))


def split_constant(matrix):
    high = matrix.astype(jnp.bfloat16)
    low = (matrix - high.astype(np.float32)).astype(jnp.bfloat16)
    return high, low


def dot(left, right, contract=((1,), (0,))):
    return lax.dot_general(left, right, (contract, ((), ())), preferred_element_type=jnp.float32)


def exact_dot(left, right, contract=((1,), (0,))):
    return lax.dot_general(
        left,
        right,
        (contract, ((), ())),
        precision=lax.Precision.HIGHEST,
        preferred_element_type=jnp.float32,
    )


def split(value, parts):
    pieces = []
    for _ in range(parts):
        piece = value.astype(jnp.bfloat16)
        pieces.append(piece)
        value = value - piece.astype(jnp.float32)
    return pieces


def filter_kernel(frames, row_bands, col_bands, out, held, planes, sems):
    count, plane_count = frames.shape[0], frames.shape[1]
    half_rows, half_cols = row_bands.shape[0] // 4, col_bands.shape[1] // 2
    copies = []
    for t in range(count):
        copy = pltpu.make_async_copy(frames.at[t], held.at[t], sems.at[t])
        copy.start()
        copies.append(copy)

    def row_pass(t):
        copies[t].wait()
        narrow, broad = [], []
        for p in range(plane_count):
            passed = dot(row_bands[...], held[t, p])
            passed = passed[: 2 * half_rows] + passed[2 * half_rows :]
            narrow.append(passed[:half_rows])
            broad.append(passed[half_rows:])
        narrow_high, narrow_low = split(jnp.concatenate(narrow, axis=0), 2)
        broad_high, broad_low = split(jnp.concatenate(broad, axis=0), 2)
        return (
            jnp.concatenate([narrow_high, broad_high], axis=1),
            jnp.concatenate([narrow_low, broad_low], axis=1),
        )

    def column_pass(t, high, low):
        wide_sum = dot(high, col_bands[...])
        low_sum = dot(low, col_bands[:, :half_cols])
        planes[:, t, :] = wide_sum[:, :half_cols] + (wide_sum[:, half_cols:] + low_sum)

    waiting = row_pass(0)
    for t in range(count):
        current, waiting = waiting, row_pass(t + 1) if t + 1 < count else None
        column_pass(t, *current)
    out[...] = planes[...].astype(jnp.bfloat16).reshape(out.shape)


def filter_call(frames, groups):
    count, plane_count, rows, cols = frames.shape
    narrow_high, narrow_low = split_constant(band_matrix(1.5, rows))
    broad_high, broad_low = split_constant(band_matrix(3.0, rows))
    row_bands = np.concatenate([narrow_high, broad_high, narrow_low, broad_low], axis=0)
    narrow_high, narrow_low = split_constant(band_matrix(1.5, cols).T)
    broad_high, broad_low = split_constant(-band_matrix(3.0, cols).T)
    col_bands = np.concatenate(
        [
            np.concatenate([narrow_high, narrow_low], axis=1),
            np.concatenate([broad_high, broad_low], axis=1),
        ],
        axis=0,
    )
    lines = plane_count * (rows // 2)
    shape = (groups, lines // groups, count, cols // 2)
    vmem = pl.BlockSpec(memory_space=pltpu.VMEM)
    return pl.pallas_call(
        filter_kernel,
        out_shape=jax.ShapeDtypeStruct(shape, jnp.bfloat16),
        in_specs=[pl.BlockSpec(memory_space=pl.ANY), vmem, vmem],
        out_specs=vmem,
        scratch_shapes=[
            pltpu.VMEM(frames.shape, jnp.bfloat16),
            pltpu.VMEM((lines, count, cols // 2), jnp.float32),
            pltpu.SemaphoreType.DMA((count,)),
        ],
        name="filter_volumes",
    )(frames, jnp.asarray(row_bands), jnp.asarray(col_bands))


def deconvolve_kernel(voxel_count, second, taps, received, deconvolved, keep, send):
    length = deconvolved.shape[0]
    taps_row = jnp.concatenate(
        [taps[...].astype(jnp.float32), jnp.zeros((1, length - taps.shape[1]), jnp.float32)], axis=1
    )
    lags = pltpu.roll(
        jnp.broadcast_to(taps_row, (length, length)), 0, 1, stride=1, stride_axis=0
    )
    source = lax.broadcasted_iota(jnp.int32, (length, length), 0)
    target = lax.broadcasted_iota(jnp.int32, (length, length), 1)
    toeplitz = jnp.where(target >= source, lags, 0.0).T.astype(jnp.bfloat16)
    if len(received.shape) == 4:
        lines = [
            received[:, r].astype(jnp.float32).reshape(length, received.shape[3]).astype(jnp.bfloat16)
            for r in range(received.shape[1])
        ]
    else:
        lines = [received[r] for r in range(received.shape[0])]
    series = dot(toeplitz, jnp.concatenate(lines, axis=1)).astype(jnp.bfloat16)
    deconvolved[...] = series
    full = dot(series, series, ((1,), (1,))) * (1.0 / voxel_count)
    half = length // 2
    row = lax.broadcasted_iota(jnp.int32, (half, half), 0)
    lane = lax.broadcasted_iota(jnp.int32, (half, half), 1)
    early, late = full[:half, :half], full[half:, half:]
    diagonal = jnp.sum(jnp.where(row == lane, early, 0.0), axis=0, keepdims=True)
    parts = (
        jnp.concatenate([full[half:, :half], jnp.broadcast_to(diagonal, (SUB, half))], axis=0),
        jnp.concatenate([jnp.where(row > lane, early, late), jnp.zeros((SUB, half))], axis=0),
    )
    for side in range(2):

        @pl.when(second[0] == side)
        def _():
            keep[...] = parts[side]
            send[...] = parts[1 - side]


def deconvolve_call(second, kernel_taps, received, voxel_count):
    groups, lines, count, width = received.shape
    length = groups * count
    if count % SUB:
        received = jnp.swapaxes(received, 0, 1).reshape(lines, length, width)
    vmem = pl.BlockSpec(memory_space=pltpu.VMEM)
    return pl.pallas_call(
        functools.partial(deconvolve_kernel, voxel_count),
        out_shape=(
            jax.ShapeDtypeStruct((length, lines * width), jnp.bfloat16),
            jax.ShapeDtypeStruct((length // 2 + SUB, length // 2), jnp.float32),
            jax.ShapeDtypeStruct((length // 2 + SUB, length // 2), jnp.float32),
        ),
        in_specs=[pl.BlockSpec(memory_space=pltpu.SMEM), vmem, vmem],
        out_specs=(vmem, vmem, vmem),
        name="deconvolve_gram",
    )(second, kernel_taps.reshape(1, -1), received)


def exchange(value, mask, size):
    return lax.ppermute(value, AXES, [(i, i ^ mask) for i in range(size)])


def sum_over_devices(keep, send, size):
    bits = size.bit_length() - 1
    half = keep + exchange(send, 1, size)
    first = [exchange(half, mask, size) for mask in (2, 4, 6)]
    half = (half + first[0]) + (first[1] + first[2])
    bit = 3
    while bit < bits:
        half = half + exchange(half, 1 << bit, size)
        if bit + 1 < bits:
            half = half + exchange(half, 3 << bit, size)
        bit += 2
    return half, exchange(half, 1, size)


def eliminate(gram):
    size = gram.shape[0]
    blocks = size // SUB
    identity = (
        lax.broadcasted_iota(jnp.int32, (size, size), 0)
        == lax.broadcasted_iota(jnp.int32, (size, size), 1)
    ).astype(jnp.float32)
    left = [gram[SUB * i : SUB * (i + 1)] for i in range(blocks)]
    right = [identity[SUB * i : SUB * (i + 1)] for i in range(blocks)]
    row = lax.broadcasted_iota(jnp.int32, (SUB, size), 0)
    lane = lax.broadcasted_iota(jnp.int32, (SUB, size), 1)

    def columns(block, k):
        return [
            jnp.broadcast_to(block[:, SUB * k + j : SUB * k + j + 1], (SUB, size))
            for j in range(SUB)
        ]

    upper, inverse = [], []
    for k in range(blocks):
        cols = columns(left[k], k)
        steps = []
        pivots = jnp.ones((SUB, size), jnp.float32)
        for j in range(SUB):
            pivot = jnp.broadcast_to(cols[j][j : j + 1], (SUB, size))
            reciprocal = 1.0 / pivot
            pivots = jnp.where(row == j, pivot, pivots)
            tops = [
                jnp.broadcast_to(cols[jj][j : j + 1], (SUB, size)) for jj in range(j + 1, SUB)
            ]
            left_row = jnp.broadcast_to(left[k][j : j + 1], (SUB, size))
            right_row = jnp.broadcast_to(right[k][j : j + 1], (SUB, size))
            ratio = jnp.where(row > j, cols[j] * reciprocal, 0.0)
            for jj in range(j + 1, SUB):
                cols[jj] = cols[jj] - ratio * tops[jj - j - 1]
            left[k] = left[k] - ratio * left_row
            right[k] = right[k] - ratio * right_row
            steps.append((reciprocal, tops, left_row, right_row))
        scale = lax.rsqrt(pivots)
        upper.append(jnp.where(lane >= row + SUB * k, left[k] * scale, 0.0))
        inverse.append(right[k] * scale)
        for i in range(k + 1, blocks):
            cols = columns(left[i], k)
            for j, (reciprocal, tops, left_row, right_row) in enumerate(steps):
                ratio = cols[j] * reciprocal
                for jj in range(j + 1, SUB):
                    cols[jj] = cols[jj] - ratio * tops[jj - j - 1]
                left[i] = left[i] - ratio * left_row
                right[i] = right[i] - ratio * right_row
    return jnp.concatenate(upper, axis=0), jnp.concatenate(inverse, axis=0)


def basis_kernel(second, mine, pairs, sketch, deconvolved, basis, factor):
    half = mine.shape[1]
    is_second = second[0] == 1
    cross = jnp.where(is_second, pairs[...], mine[...])
    square = jnp.where(is_second, mine[:half], pairs[:half])
    corner, diagonal = cross[:half], cross[half : half + 1]
    row = lax.broadcasted_iota(jnp.int32, (half, half), 0)
    lane = lax.broadcasted_iota(jnp.int32, (half, half), 1)
    turned = square.T
    early = jnp.where(row > lane, square, jnp.where(row < lane, turned, diagonal))
    late = jnp.where(row > lane, turned, square)
    data_gram = jnp.concatenate(
        [
            jnp.concatenate([early, corner.T], axis=1),
            jnp.concatenate([corner, late], axis=1),
        ],
        axis=0,
    )
    weights = sketch[...]
    high, middle, low = split(data_gram, 3)
    weighted = dot(high, weights) + (dot(middle, weights) + dot(low, weights))
    high, middle, low = split(weighted, 3)
    rows_first = ((0,), (0,))
    gram = dot(weights, high, rows_first) + (
        dot(weights, middle, rows_first) + dot(weights, low, rows_first)
    )
    _, inverse = eliminate(gram)
    projected = exact_dot(inverse, weighted, ((1,), (1,)))
    gram = exact_dot(exact_dot(projected, data_gram), projected, ((1,), (1,)))
    upper, inverse = eliminate(gram)
    factor[...] = upper
    high, middle, low = split(exact_dot(inverse, projected), 3)
    series = deconvolved[...]
    basis[...] = dot(high, series) + (dot(middle, series) + dot(low, series))


def basis_call(second, mine, pairs, sketch, deconvolved):
    rank = sketch.shape[1]
    vmem = pl.BlockSpec(memory_space=pltpu.VMEM)
    return pl.pallas_call(
        basis_kernel,
        out_shape=(
            jax.ShapeDtypeStruct((rank, deconvolved.shape[1]), jnp.float32),
            jax.ShapeDtypeStruct((rank, rank), jnp.float32),
        ),
        in_specs=[pl.BlockSpec(memory_space=pltpu.SMEM)] + [vmem] * 4,
        out_specs=(vmem, vmem),
        name="orthonormal_basis",
    )(second, mine, pairs, sketch, deconvolved)


def shards(size, frames, sketch, kernel_taps):
    voxel_count = frames.shape[1] * (frames.shape[2] // 2) * (frames.shape[3] // 2)
    filtered = filter_call(frames, size)
    received = lax.all_to_all(filtered, AXES, split_axis=0, concat_axis=0, tiled=True)
    second = (lax.axis_index(AXES) % 2).astype(jnp.int32).reshape(1)
    deconvolved, keep, send = deconvolve_call(second, kernel_taps, received, voxel_count)
    mine, pairs = sum_over_devices(keep, send, size)
    return basis_call(second, mine, pairs, sketch, deconvolved)


def solution(mesh):
    size = mesh.shape["wide"] * mesh.shape["narrow"]
    return jax.shard_map(
        functools.partial(shards, size),
        mesh=mesh,
        in_specs=(P(AXES, None, None, None), P(), P()),
        out_specs=(P(None, AXES), P()),
        check_vma=False,
    )
```

```python
import functools

import jax
import jax.numpy as jnp
import numpy as np
from jax import lax
from jax.experimental import pallas as pl
from jax.experimental.pallas import tpu as pltpu
from jax.sharding import PartitionSpec as P

AXES = ("wide", "narrow")
SUB = 8
LANES = 128


def gauss_taps(spread):
    position = np.arange(15, dtype=np.float32) - np.float32(7.0)
    weights = np.exp(-position * position / np.float32(2.0 * spread * spread))
    return (weights / np.sum(weights, dtype=np.float32)).astype(np.float32)


def band_matrix(spread, length):
    outputs = length // 2
    offset = np.arange(length)[None, :] - 2 * np.arange(outputs)[:, None] + 7
    weights = gauss_taps(spread)
    inside = (offset >= 0) & (offset < 15)
    return np.where(inside, weights[np.clip(offset, 0, 14)], np.float32(0.0))


def split_constant(matrix):
    high = matrix.astype(jnp.bfloat16)
    low = (matrix - high.astype(np.float32)).astype(jnp.bfloat16)
    return high, low


def on_chip(value):
    return pltpu.with_memory_space_constraint(value, pltpu.VMEM)


PARAMS = pltpu.CompilerParams(vmem_limit_bytes=32 << 20)


def dot(left, right, contract=((1,), (0,))):
    return lax.dot_general(left, right, (contract, ((), ())), preferred_element_type=jnp.float32)


def exact_dot(left, right, contract=((1,), (0,))):
    return lax.dot_general(
        left,
        right,
        (contract, ((), ())),
        precision=lax.Precision.HIGHEST,
        preferred_element_type=jnp.float32,
    )


def split(value, parts):
    pieces = []
    for _ in range(parts):
        piece = value.astype(jnp.bfloat16)
        pieces.append(piece)
        value = value - piece.astype(jnp.float32)
    return pieces


def filter_kernel(frames, row_taps, col_taps, out, held, row_bands, col_bands, planes, sems):
    count, plane_count = frames.shape[0], frames.shape[1]
    half_rows, half_cols = row_bands.shape[0] // 4, col_bands.shape[1] // 2
    copies = [pltpu.make_async_copy(frames.at[t], held.at[t], sems.at[t]) for t in range(count)]
    row_copy = pltpu.make_async_copy(row_taps, row_bands, sems.at[count])
    col_copy = pltpu.make_async_copy(col_taps, col_bands, sems.at[count + 1])
    for copy in [row_copy, copies[0], col_copy] + copies[1:]:
        copy.start()
    row_copy.wait()

    def row_pass(t):
        copies[t].wait()
        narrow, broad = [], []
        for p in range(plane_count):
            passed = dot(row_bands[...], held[t, p])
            passed = passed[: 2 * half_rows] + passed[2 * half_rows :]
            narrow.append(passed[:half_rows])
            broad.append(passed[half_rows:])
        narrow_high, narrow_low = split(jnp.concatenate(narrow, axis=0), 2)
        broad_high, broad_low = split(jnp.concatenate(broad, axis=0), 2)
        return (
            jnp.concatenate([narrow_high, broad_high], axis=1),
            jnp.concatenate([narrow_low, broad_low], axis=1),
        )

    def column_pass(t, high, low):
        wide_sum = dot(high, col_bands[...])
        low_sum = dot(low, col_bands[:, :half_cols])
        planes[:, t, :] = wide_sum[:, :half_cols] + (wide_sum[:, half_cols:] + low_sum)

    waiting = row_pass(0)
    col_copy.wait()
    for t in range(count):
        current, waiting = waiting, row_pass(t + 1) if t + 1 < count else None
        column_pass(t, *current)
    out[...] = planes[...].astype(jnp.bfloat16).reshape(out.shape)


def filter_call(frames, groups):
    count, plane_count, rows, cols = frames.shape
    narrow_high, narrow_low = split_constant(band_matrix(1.5, rows))
    broad_high, broad_low = split_constant(band_matrix(3.0, rows))
    row_bands = np.concatenate([narrow_high, broad_high, narrow_low, broad_low], axis=0)
    narrow_high, narrow_low = split_constant(band_matrix(1.5, cols).T)
    broad_high, broad_low = split_constant(-band_matrix(3.0, cols).T)
    col_bands = np.concatenate(
        [
            np.concatenate([narrow_high, narrow_low], axis=1),
            np.concatenate([broad_high, broad_low], axis=1),
        ],
        axis=0,
    )
    lines = plane_count * (rows // 2)
    shape = (groups, lines // groups, count, cols // 2)
    off_chip = pl.BlockSpec(memory_space=pltpu.HBM)
    return pl.pallas_call(
        filter_kernel,
        out_shape=pltpu.VMEM(shape, jnp.bfloat16),
        in_specs=[off_chip] * 3,
        out_specs=pl.BlockSpec(memory_space=pltpu.VMEM),
        scratch_shapes=[
            pltpu.VMEM(frames.shape, jnp.bfloat16),
            pltpu.VMEM(row_bands.shape, jnp.bfloat16),
            pltpu.VMEM(col_bands.shape, jnp.bfloat16),
            pltpu.VMEM((lines, count, cols // 2), jnp.float32),
            pltpu.SemaphoreType.DMA((count + 2,)),
        ],
        name="filter_volumes",
    )(frames, jnp.asarray(row_bands), jnp.asarray(col_bands))


def deconvolve_kernel(voxel_count, second, taps, received, deconvolved, keep, send):
    length = deconvolved.shape[0]
    taps_row = jnp.concatenate(
        [taps[...].astype(jnp.float32), jnp.zeros((1, length - taps.shape[1]), jnp.float32)], axis=1
    )
    lags = pltpu.roll(
        jnp.broadcast_to(taps_row, (length, length)), 0, 1, stride=1, stride_axis=0
    )
    source = lax.broadcasted_iota(jnp.int32, (length, length), 0)
    target = lax.broadcasted_iota(jnp.int32, (length, length), 1)
    toeplitz = jnp.where(target >= source, lags, 0.0).T.astype(jnp.bfloat16)
    if len(received.shape) == 4:
        lines = [
            received[:, r].astype(jnp.float32).reshape(length, received.shape[3]).astype(jnp.bfloat16)
            for r in range(received.shape[1])
        ]
    else:
        lines = [received[r] for r in range(received.shape[0])]
    series = dot(toeplitz, jnp.concatenate(lines, axis=1)).astype(jnp.bfloat16)
    deconvolved[...] = series
    full = dot(series, series, ((1,), (1,))) * (1.0 / voxel_count)
    half = length // 2
    row = lax.broadcasted_iota(jnp.int32, (half, half), 0)
    lane = lax.broadcasted_iota(jnp.int32, (half, half), 1)
    early, late = full[:half, :half], full[half:, half:]
    diagonal = jnp.sum(jnp.where(row == lane, early, 0.0), axis=0, keepdims=True)
    parts = (
        jnp.concatenate([full[half:, :half], jnp.broadcast_to(diagonal, (SUB, half))], axis=0),
        jnp.concatenate([jnp.where(row > lane, early, late), jnp.zeros((SUB, half))], axis=0),
    )
    for side in range(2):

        @pl.when(second[0] == side)
        def _():
            keep[...] = parts[side]
            send[...] = parts[1 - side]


def deconvolve_call(second, kernel_taps, received, voxel_count):
    groups, lines, count, width = received.shape
    length = groups * count
    if count % SUB:
        received = jnp.swapaxes(received, 0, 1).reshape(lines, length, width)
    vmem = pl.BlockSpec(memory_space=pltpu.VMEM)
    return pl.pallas_call(
        functools.partial(deconvolve_kernel, voxel_count),
        out_shape=(
            pltpu.VMEM((length, lines * width), jnp.bfloat16),
            pltpu.VMEM((length // 2 + SUB, length // 2), jnp.float32),
            pltpu.VMEM((length // 2 + SUB, length // 2), jnp.float32),
        ),
        in_specs=[pl.BlockSpec(memory_space=pltpu.SMEM), vmem, vmem],
        out_specs=(vmem, vmem, vmem),
        compiler_params=PARAMS,
        name="deconvolve_gram",
    )(second, kernel_taps.reshape(1, -1), on_chip(received))


def exchange(value, mask, size):
    return lax.ppermute(value, AXES, [(i, i ^ mask) for i in range(size)])


def sum_over_devices(keep, send, size):
    bits = size.bit_length() - 1
    half = keep + exchange(send, 1, size)
    first = [exchange(half, mask, size) for mask in (2, 4, 6)]
    half = (half + first[0]) + (first[1] + first[2])
    bit = 3
    while bit < bits:
        half = half + exchange(half, 1 << bit, size)
        if bit + 1 < bits:
            half = half + exchange(half, 3 << bit, size)
        bit += 2
    return half, exchange(half, 1, size)


def eliminate(gram):
    size = gram.shape[0]
    blocks = size // SUB
    identity = (
        lax.broadcasted_iota(jnp.int32, (size, size), 0)
        == lax.broadcasted_iota(jnp.int32, (size, size), 1)
    ).astype(jnp.float32)
    left = [gram[SUB * i : SUB * (i + 1)] for i in range(blocks)]
    right = [identity[SUB * i : SUB * (i + 1)] for i in range(blocks)]
    row = lax.broadcasted_iota(jnp.int32, (SUB, size), 0)
    lane = lax.broadcasted_iota(jnp.int32, (SUB, size), 1)

    def columns(block, k):
        return [
            jnp.broadcast_to(block[:, SUB * k + j : SUB * k + j + 1], (SUB, size))
            for j in range(SUB)
        ]

    upper, inverse = [], []
    for k in range(blocks):
        cols = columns(left[k], k)
        steps = []
        pivots = jnp.ones((SUB, size), jnp.float32)
        for j in range(SUB):
            pivot = jnp.broadcast_to(cols[j][j : j + 1], (SUB, size))
            reciprocal = 1.0 / pivot
            pivots = jnp.where(row == j, pivot, pivots)
            tops = [
                jnp.broadcast_to(cols[jj][j : j + 1], (SUB, size)) for jj in range(j + 1, SUB)
            ]
            left_row = jnp.broadcast_to(left[k][j : j + 1], (SUB, size))
            right_row = jnp.broadcast_to(right[k][j : j + 1], (SUB, size))
            ratio = jnp.where(row > j, cols[j] * reciprocal, 0.0)
            for jj in range(j + 1, SUB):
                cols[jj] = cols[jj] - ratio * tops[jj - j - 1]
            left[k] = left[k] - ratio * left_row
            right[k] = right[k] - ratio * right_row
            steps.append((reciprocal, tops, left_row, right_row))
        scale = lax.rsqrt(pivots)
        upper.append(jnp.where(lane >= row + SUB * k, left[k] * scale, 0.0))
        inverse.append(right[k] * scale)
        for i in range(k + 1, blocks):
            cols = columns(left[i], k)
            for j, (reciprocal, tops, left_row, right_row) in enumerate(steps):
                ratio = cols[j] * reciprocal
                for jj in range(j + 1, SUB):
                    cols[jj] = cols[jj] - ratio * tops[jj - j - 1]
                left[i] = left[i] - ratio * left_row
                right[i] = right[i] - ratio * right_row
    return jnp.concatenate(upper, axis=0), jnp.concatenate(inverse, axis=0)


def basis_kernel(second, mine, pairs, sketch, deconvolved, basis, factor):
    half = mine.shape[1]
    is_second = second[0] == 1
    cross = jnp.where(is_second, pairs[...], mine[...])
    square = jnp.where(is_second, mine[:half], pairs[:half])
    corner, diagonal = cross[:half], cross[half : half + 1]
    row = lax.broadcasted_iota(jnp.int32, (half, half), 0)
    lane = lax.broadcasted_iota(jnp.int32, (half, half), 1)
    turned = square.T
    early = jnp.where(row > lane, square, jnp.where(row < lane, turned, diagonal))
    late = jnp.where(row > lane, turned, square)
    data_gram = jnp.concatenate(
        [
            jnp.concatenate([early, corner.T], axis=1),
            jnp.concatenate([corner, late], axis=1),
        ],
        axis=0,
    )
    weights = sketch[...]
    high, middle, low = split(data_gram, 3)
    weighted = dot(high, weights) + (dot(middle, weights) + dot(low, weights))
    high, middle, low = split(weighted, 3)
    rows_first = ((0,), (0,))
    gram = dot(weights, high, rows_first) + (
        dot(weights, middle, rows_first) + dot(weights, low, rows_first)
    )
    _, inverse = eliminate(gram)
    projected = exact_dot(inverse, weighted, ((1,), (1,)))
    gram = exact_dot(exact_dot(projected, data_gram), projected, ((1,), (1,)))
    upper, inverse = eliminate(gram)
    factor[...] = upper
    high, middle, low = split(exact_dot(inverse, projected), 3)
    series = deconvolved[...]
    basis[...] = dot(high, series) + (dot(middle, series) + dot(low, series))


def basis_call(second, mine, pairs, sketch, deconvolved):
    rank = sketch.shape[1]
    vmem = pl.BlockSpec(memory_space=pltpu.VMEM)
    return pl.pallas_call(
        basis_kernel,
        out_shape=(
            jax.ShapeDtypeStruct((rank, deconvolved.shape[1]), jnp.float32),
            jax.ShapeDtypeStruct((rank, rank), jnp.float32),
        ),
        in_specs=[pl.BlockSpec(memory_space=pltpu.SMEM)] + [vmem] * 4,
        out_specs=(vmem, vmem),
        compiler_params=PARAMS,
        name="orthonormal_basis",
    )(second, on_chip(mine), on_chip(pairs), sketch, on_chip(deconvolved))


def shards(size, frames, sketch, kernel_taps):
    voxel_count = frames.shape[1] * (frames.shape[2] // 2) * (frames.shape[3] // 2)
    filtered = filter_call(frames, size)
    received = lax.all_to_all(filtered, AXES, split_axis=0, concat_axis=0, tiled=True)
    second = (lax.axis_index(AXES) % 2).astype(jnp.int32).reshape(1)
    deconvolved, keep, send = deconvolve_call(second, kernel_taps, received, voxel_count)
    mine, pairs = sum_over_devices(keep, send, size)
    return basis_call(second, mine, pairs, sketch, deconvolved)


def solution(mesh):
    size = mesh.shape["wide"] * mesh.shape["narrow"]
    return jax.shard_map(
        functools.partial(shards, size),
        mesh=mesh,
        in_specs=(P(AXES, None, None, None), P(), P()),
        out_specs=(P(None, AXES), P()),
        check_vma=False,
    )
```
